32 devices in a mesh: ctx: 8 (over z, y), head: 4 (over x, core).
Axes of the slice: x: 2, y: 2, z: 4, core: 2. Of those that a mesh axis runs over, the one named last changes fastest.
Arguments:
- query: bfloat16 [2048, 4096], P('ctx', 'head'), may hold values from -6 to 6
- key: bfloat16 [2048, 4096], P('ctx', 'head'), may hold values from -6 to 6
- value: bfloat16 [2048, 4096], P('ctx', 'head'), may hold values from -6 to 6
- episode_lengths: int32 [8], replicated, may hold values from 1 to 1024, 2048 in all
- attn_gain: float32 [4096], P('head'), may hold values from 0.1 to 1.9
- out_weight: bfloat16 [4096, 3072], P('head', 'ctx'), may hold values from -0.09375 to 0.09375
- residual: bfloat16 [2048, 3072], P('ctx', 'head'), may hold values from -36 to 36
- norm_gain: float32 [3072], P('head'), may hold values from 0.1 to 1.9
- expert_ids: int32 [2048, 2], P('ctx'), may hold values from 0 to 7, all different within a row; in each aligned block of 256 rows (0 to 255, 256 to 511, ...) at most 96 rows name the same one
- route_weights: int32 [2048, 2], P('ctx'), may hold values from 4096 to 65535
- gate_weight: bfloat16 [8, 3072, 5120], P('ctx', None, 'head'), may hold values from -0.109375 to 0.109375
- up_weight: bfloat16 [8, 3072, 5120], P('ctx', None, 'head'), may hold values from -0.109375 to 0.109375
- down_weight: bfloat16 [8, 5120, 3072], P('ctx', 'head'), may hold values from -0.125 to 0.125
Outputs:
- layer_out: bfloat16 [2048, 3072], P('ctx', 'head')
The draws below stay inside these ranges and needn't reach their ends.
Inputs may be any that keep to these rules, and one draw needn't show every extreme that they name: `expert_ids`: in the rows of one device (256 tokens) no expert is named by more than 96 rows, a bound that some block reaches; a row names two different experts.
All inputs are finite; a program needn't handle non-finite values.
Results may differ from the reference program's by a relative error of at most 0.012.
Values may be sent and summed in bfloat16 or wider, within the bound.
A program may use at most 128 MiB of HBM per device.

```python
import math
import jax
import jax.numpy as jnp
import numpy as np
from jax import lax

D = 3072
HEADS = 32
HEAD_DIM = 128
FF = 5120
TOK_DEV = 256
EPISODES = 8
HQ = 4096
EXPERTS = 8
TOKENS = 2048
CAP = 96
N_HEAD = 4


def draw_residual(key, part):
    first, second, third = jax.random.split(key, 3)
    base = jnp.clip(jax.random.normal(first, (TOKENS, D), jnp.float32), -4.0, 4.0)
    rows = jnp.exp(jax.random.uniform(second, (TOKENS, 1), jnp.float32, math.log(0.3), math.log(3.0)))
    columns = jnp.exp(jax.random.uniform(third, (1, D), jnp.float32, math.log(0.3), math.log(3.0)))
    return (base * rows * columns).astype(jnp.bfloat16)


def set_ends(entries, own_key, least, top_value):
    index_at = [jax.random.randint(jax.random.fold_in(own_key, axis), (), 0, length) for axis, length in enumerate(entries.shape)]
    main_axis = entries.shape.index(max(entries.shape))
    neighbour = index_at[:main_axis] + [(index_at[main_axis] + 1) % entries.shape[main_axis]] + index_at[main_axis + 1:]
    return entries.at[tuple(index_at)].set(least).at[tuple(neighbour)].set(top_value)


def with_spikes(result, key, source, target, parts, factor):
    owner, partner = [(jnp.arange(result.shape[axis_at]) // (result.shape[axis_at] // parts)).reshape([-1 if axis == axis_at else 1 for axis in range(result.ndim)]) for axis_at in (source, target)]
    chosen = jax.random.permutation(key, parts)[partner]
    strong = (owner == chosen) | (owner == (partner + parts // 2) % parts)
    return jnp.where(strong, factor * result, result)


def shard_levels(own_key, dims, pieces, low, high):
    level, own = 1.0, jax.random.fold_in(own_key, 6)
    for position, blocks in pieces:
        draws = jnp.exp(jax.random.uniform(jax.random.fold_in(own, position), (blocks,), jnp.float32, low / len(pieces), high / len(pieces)))
        level = level * jnp.repeat(draws, dims[position] // blocks).reshape([-1 if axis == position else 1 for axis in range(len(dims))])
    return level


def length_profile(amount, total, bound, skew):
    portions = [(1 << 20) // math.isqrt(rank ** skew) + 1 for rank in range(2, amount + 1)]
    rest, counts = total - bound - (amount - 1), [1] * (amount - 1)
    while rest > 0:
        candidates = [i for i in range(amount - 1) if counts[i] < bound]
        pool, remaining = sum([portions[i] for i in candidates]), rest
        for i in candidates:
            extra = min(bound - counts[i], max(1, remaining * portions[i] // pool), rest)
            counts[i] = counts[i] + extra
            rest = rest - extra
    return np.array([bound] + counts)


def uneven_parts(key, amount, total, most, lean):
    if amount == 2:
        one = jax.random.randint(key, (), max(1, total - most), min(most, total - 1) + 1)
        return jnp.stack([one, total - one])
    sizes = jnp.asarray(length_profile(amount, total, most, lean), jnp.int32)
    pairs = (amount - 1) // 2
    giver, taker = sizes[1:1 + 2 * pairs:2], sizes[2:2 + 2 * pairs:2]
    slack = jnp.minimum(giver - 1, most - taker)
    passed = jax.random.randint(jax.random.fold_in(key, 1), (pairs,), 0, 1 << 20) % (slack + 1)
    sizes = sizes.at[1:1 + 2 * pairs:2].set(giver - passed).at[2:2 + 2 * pairs:2].set(taker + passed)
    return sizes[jax.random.permutation(jax.random.fold_in(key, 2), amount)]


def routed_block(own_key, own, number, rows, number_of, top, limit, slope):
    sequence = jax.random.permutation(own_key, number_of)
    packed, ordinary = load_shares(number_of, rows * top, limit, slope, True), load_shares(number_of, rows * top, limit, slope, False)
    places = jnp.arange(number_of)

    def named(sizes, turn):
        used = int((sizes > 0).sum())
        fixed = max(1, used // 4)
        moved = fixed + (places - fixed + turn * (used - fixed)) % max(1, number_of - fixed)
        return jnp.zeros((number_of,), jnp.int32).at[sequence[jnp.where(places < fixed, places, moved)]].set(jnp.asarray(sizes, jnp.int32))

    sizes = jnp.where(number % 4 == 0, named(packed, number // 4), named(ordinary, number - number // 4 - 1))
    mixed = jax.random.permutation(jax.random.fold_in(own, 3), number_of)
    donor, taker = mixed[0:number_of // 2 * 2:2], mixed[1:number_of // 2 * 2:2]
    slack = jnp.minimum(sizes[donor] - 1, limit - sizes[taker]) // 2
    slack = jnp.where((donor == sequence[0]) | (taker == sequence[0]) | (sizes[taker] == 0), 0, jnp.maximum(slack, 0))
    moved = jax.random.randint(jax.random.fold_in(own, 4), (number_of // 2,), 0, 1 << 20) % (slack + 1)
    sizes = sizes.at[donor].add(-moved).at[taker].add(moved)
    labels = jnp.searchsorted(jnp.cumsum(sizes), jnp.arange(rows * top), side="right").astype(jnp.int32)
    listing = labels.reshape(top, rows).T
    listing = listing[jax.random.permutation(jax.random.fold_in(own, 1), rows)]
    turn = jax.random.randint(jax.random.fold_in(own, 2), (rows, 1), 0, top)
    return jnp.take_along_axis(listing, (jnp.arange(top)[None, :] + turn) % top, axis=1)


def load_shares(count, total, bound, slope, full):
    loads = [(1 << 20) // math.isqrt(rank ** slope) + 1 for rank in range(1, count + 1)]
    largest = bound if full else min(bound, max(-(-total // count), total * loads[0] // sum(loads)))
    least = 1 if total - largest >= count - 1 else 0
    holding, spare = [largest] + [least] * (count - 1), total - largest - least * (count - 1)
    while spare > 0:
        candidates = [i for i in range(1, count) if holding[i] < largest] or [i for i in range(1, count) if holding[i] < bound]
        pool, budget = sum([loads[i] for i in candidates]), spare
        for i in candidates:
            extra = min(bound - holding[i], max(1, budget * loads[i] // pool), spare)
            holding[i] = holding[i] + extra
            spare = spare - extra
    return np.array(holding)


def normal_values(rng, dims, spread, limit, pieces=(), held_as=jnp.bfloat16):
    entries = jax.random.normal(rng, dims, jnp.float32) * spread
    if len(pieces) > 0:
        entries = shard_levels(rng, dims, pieces, -0.22, 0.18) * entries
    return jnp.clip(entries, min=-limit, max=limit).astype(held_as)


def noise_with(rng, dims, spread, limit, pieces, heavy, kind=jnp.bfloat16):
    values = spread * jax.random.normal(rng, dims, jnp.float32)
    if pieces:
        values = values * shard_levels(rng, dims, pieces, -0.22, 0.18)
    return jnp.clip(with_spikes(values, jax.random.fold_in(rng, 3), *heavy), -limit, limit).astype(kind)


def setup_inputs(seed: int = 0) -> dict:
    splits = jax.random.split(jax.random.key(seed), 14)
    query = normal_values(splits[0], (TOKENS, HQ), 1.0, 6.0, ((0, 8), (1, 4)))
    key = normal_values(splits[1], (TOKENS, HQ), 1.0, 6.0, ((0, 8), (1, 4)))
    value = normal_values(splits[2], (TOKENS, HQ), 1.0, 6.0, ((0, 8), (1, 4)))
    episode_lengths = uneven_parts(splits[3], EPISODES, TOKENS, TOKENS // 2, 2).astype(jnp.int32)
    attn_gain = jnp.clip(1.0 + 0.18 * jax.random.normal(splits[4], (HQ,), jnp.float32), 0.1, 1.9)
    out_weight = normal_values(splits[5], (HQ, D), HQ ** -0.5, 0.09375, ((0, 4), (1, 8)))
    residual = draw_residual(jax.random.fold_in(splits[13], 71), 0)
    norm_gain = jnp.clip(1.0 + 0.18 * jax.random.normal(splits[7], (D,), jnp.float32), 0.1, 1.9)
    expert_ids_keys = jax.random.split(jax.random.fold_in(splits[8], 1), TOKENS // TOK_DEV)
    expert_ids_turns = jax.random.permutation(jax.random.fold_in(splits[8], 3), TOKENS // TOK_DEV)
    expert_ids = jax.vmap(lambda own, number: routed_block(jax.random.fold_in(splits[8], 2), own, number, TOK_DEV, EXPERTS, 2, CAP, 2))(expert_ids_keys, expert_ids_turns).reshape((TOKENS, 2))
    route_weights = set_ends(jax.random.randint(splits[9], (TOKENS, 2), 4096, 65536), jax.random.fold_in(splits[9], 1), 4096, 65535).astype(jnp.int32)
    gate_weight = normal_values(splits[10], (EXPERTS, D, FF), D ** -0.5, 0.109375, ((0, 8), (2, 4)))
    up_weight = normal_values(splits[11], (EXPERTS, D, FF), D ** -0.5, 0.109375, ((0, 8), (2, 4)))
    down_weight = noise_with(splits[12], (EXPERTS, FF, D), FF ** -0.5, 0.125, ((0, 8), (1, 4)), (1, 2, 4, 2.0))
    return dict(query=query, key=key, value=value, episode_lengths=episode_lengths, attn_gain=attn_gain, out_weight=out_weight, residual=residual, norm_gain=norm_gain, expert_ids=expert_ids, route_weights=route_weights, gate_weight=gate_weight, up_weight=up_weight, down_weight=down_weight)


def episode_of(positions, lengths):
    starts = (jnp.cumsum(lengths) - lengths).astype(jnp.int32)
    return (lax.optimization_barrier(jnp.sum((starts[None, :] <= positions[:, None]).astype(jnp.int32), axis=1)) - 1).astype(jnp.int32)

def attention(query, key, value, episode_lengths, attn_gain):
    total = query.shape[0]
    blocks = total // TOK_DEV
    positions = jnp.arange(total, dtype=jnp.int32)
    episode = episode_of(positions, episode_lengths)
    lifted_query = jax.nn.silu(query.astype(jnp.float32)).reshape(blocks, TOK_DEV, HEADS, HEAD_DIM)
    lifted_key = jax.nn.silu(key.astype(jnp.float32)).reshape(blocks, TOK_DEV, HEADS, HEAD_DIM)
    value_rows = value.astype(jnp.float32).reshape(blocks, TOK_DEV, HEADS, HEAD_DIM)
    episode_blocks = episode.reshape(blocks, TOK_DEV)
    order = jnp.arange(TOK_DEV, dtype=jnp.int32)
    causal = order[:, None] >= order[None, :]
    highest = lax.Precision.HIGHEST

    def advance(carry, inputs):
        state, prior = carry
        block_query, block_key, block_value, block_episode = inputs
        allowed = (causal & (block_episode[:, None] == block_episode[None, :])).astype(jnp.float32)
        scores = jnp.einsum('thd,shd->hts', block_query, block_key, precision=highest)
        inside = jnp.einsum('hts,shd->thd', scores * allowed[None], block_value, precision=highest)
        carry_mask = (block_episode == prior).astype(jnp.float32)
        outside = jnp.einsum('thd,hde->the', block_query, state, precision=highest)
        final = block_episode[-1].astype(jnp.int32)
        keep = (block_episode == final).astype(jnp.float32)
        fresh = jnp.einsum('shd,she->hde', block_key * keep[:, None, None], block_value, precision=highest)
        state = jnp.where(final == prior, state + fresh, fresh)
        return ((state, final), inside + outside * carry_mask[:, None, None])
    start_state = (jnp.zeros((HEADS, HEAD_DIM, HEAD_DIM), jnp.float32), jnp.array(-1, jnp.int32))
    _, outputs = lax.scan(advance, start_state, (lifted_query, lifted_key, value_rows, episode_blocks))
    attn = outputs.reshape(total, HEADS, HEAD_DIM)
    mean_square = lax.optimization_barrier(jnp.mean(attn * attn, axis=2, keepdims=True))
    scaled = attn * lax.rsqrt(mean_square + 1e-06) * attn_gain.reshape(HEADS, HEAD_DIM)
    return scaled.reshape(total, HQ).astype(jnp.bfloat16)

def reference(query, key, value, episode_lengths, attn_gain, out_weight, residual, norm_gain, expert_ids, route_weights, gate_weight, up_weight, down_weight):
    headed = attention(query, key, value, episode_lengths, attn_gain)
    mixed = jnp.dot(headed, out_weight, preferred_element_type=jnp.float32)
    hidden_state = residual.astype(jnp.float32) + mixed
    mean_square = lax.optimization_barrier(jnp.mean(hidden_state * hidden_state, axis=1, keepdims=True))
    normed = (hidden_state * lax.rsqrt(mean_square + 1e-06) * norm_gain).astype(jnp.bfloat16)
    raw_weights = route_weights.astype(jnp.float32)
    share = (raw_weights / lax.optimization_barrier(jnp.sum(raw_weights, axis=1, keepdims=True))).reshape(-1)
    flat_ids = expert_ids.reshape(-1)
    pair_rows = jnp.arange(flat_ids.shape[0], dtype=jnp.int32) // 2
    room = EXPERTS * CAP
    slice_width = FF // N_HEAD

    def expert_step(total, inputs):
        expert, gate_one, up_one, down_one = inputs
        matches = flat_ids == expert
        chosen = jnp.nonzero(matches, size=room, fill_value=0)[0].astype(jnp.int32)
        count = jnp.sum(matches.astype(jnp.int32)).astype(jnp.int32)
        valid = (jnp.arange(room, dtype=jnp.int32) < count).astype(jnp.float32)
        rows = normed[pair_rows[chosen]]
        gate = jnp.dot(rows, gate_one, preferred_element_type=jnp.float32)
        up = jnp.dot(rows, up_one, preferred_element_type=jnp.float32)
        gated = (jax.nn.silu(gate) * up).astype(jnp.bfloat16)
        combined = jnp.zeros((room, D), jnp.float32)
        for part_index in range(N_HEAD):
            lower = part_index * slice_width
            upper = lower + slice_width
            partial_value = jnp.dot(gated[:, lower:upper], down_one[lower:upper], preferred_element_type=jnp.float32).astype(jnp.bfloat16)
            combined = combined + partial_value.astype(jnp.float32)
        contribution = combined * (share[chosen] * valid)[:, None]
        total = total.at[pair_rows[chosen]].add(contribution)
        return (total, None)
    experts_list = jnp.arange(EXPERTS, dtype=jnp.int32)
    moe, _ = lax.scan(expert_step, jnp.zeros((TOKENS, D), jnp.float32), (experts_list, gate_weight, up_weight, down_weight))
    return (hidden_state + moe).astype(jnp.bfloat16)
```

```python
import jax
import jax.numpy as jnp
from jax import lax
from jax.sharding import PartitionSpec as P

HEAD_DIM = 128


highest = lax.Precision.HIGHEST


def episode_of(positions, lengths):
    starts = jnp.cumsum(lengths) - lengths
    return jnp.sum((starts[None, :] <= positions[:, None]).astype(jnp.int32), axis=1) - 1


def on_device(
    query,
    key,
    value,
    episode_lengths,
    attn_gain,
    out_weight,
    residual,
    norm_gain,
    expert_ids,
    route_weights,
    gate_weight,
    up_weight,
    down_weight,
):
    tok_rows = query.shape[0]
    head_size = HEAD_DIM
    heads_local = query.shape[1] // head_size
    own_index = lax.axis_index("ctx")
    ctx_count = lax.axis_size("ctx")
    positions = own_index * tok_rows + jnp.arange(tok_rows, dtype=jnp.int32)
    episode = episode_of(positions, episode_lengths)
    prior = episode_of(positions[:1] - 1, episode_lengths)[0]
    final = episode[-1]
    lifted_query = jax.nn.silu(query.astype(jnp.float32)).reshape(tok_rows, heads_local, head_size)
    lifted_key = jax.nn.silu(key.astype(jnp.float32)).reshape(tok_rows, heads_local, head_size)
    value_rows = value.astype(jnp.float32).reshape(tok_rows, heads_local, head_size)
    keep = (episode == final).astype(jnp.float32)
    state = jnp.einsum(
        "shd,she->hde", lifted_key * keep[:, None, None], value_rows, precision=highest
    )
    finals = episode_of(
        (jnp.arange(ctx_count, dtype=jnp.int32) + 1) * tok_rows - 1, episode_lengths
    )
    earlier = (jnp.arange(ctx_count) < own_index) & (finals == prior)
    gathered = lax.all_gather(state.astype(jnp.bfloat16), "ctx")
    carry_state = jnp.sum(
        jnp.where(earlier[:, None, None, None], gathered.astype(jnp.float32), 0.0), axis=0
    )
    order = jnp.arange(tok_rows, dtype=jnp.int32)
    allowed = ((order[:, None] >= order[None, :]) & (episode[:, None] == episode[None, :])).astype(
        jnp.float32
    )
    scores = jnp.einsum("thd,shd->hts", lifted_query, lifted_key, precision=highest)
    inside = jnp.einsum("hts,shd->thd", scores * allowed[None], value_rows, precision=highest)
    outside = jnp.einsum("thd,hde->the", lifted_query, carry_state, precision=highest)
    attn = inside + outside * (episode == prior).astype(jnp.float32)[:, None, None]
    mean_square = jnp.mean(attn * attn, axis=2, keepdims=True)
    scaled = attn * lax.rsqrt(mean_square + 1e-06) * attn_gain.reshape(heads_local, head_size)
    headed = scaled.reshape(tok_rows, heads_local * head_size).astype(jnp.bfloat16)
    mixed_part = jnp.dot(
        headed,
        lax.all_gather(out_weight, "ctx", axis=1, tiled=True),
        preferred_element_type=jnp.float32,
    )
    width = mixed_part.shape[1]
    mixed_slice = lax.psum_scatter(
        mixed_part.astype(jnp.bfloat16), "head", scatter_dimension=1, tiled=True
    ).astype(jnp.float32)
    hidden_slice = residual.astype(jnp.float32) + mixed_slice
    squares = lax.psum(jnp.sum(hidden_slice * hidden_slice, axis=1), "head")
    normed = (hidden_slice * lax.rsqrt(squares / width + 1e-06)[:, None] * norm_gain).astype(
        jnp.bfloat16
    )
    experts_count = gate_weight.shape[0] * ctx_count
    capacity = 3 * tok_rows // experts_count
    flat_ids = expert_ids.reshape(-1)
    onehot = (flat_ids[:, None] == jnp.arange(experts_count, dtype=jnp.int32)[None, :]).astype(
        jnp.int32
    )
    slot = jnp.sum(jnp.cumsum(onehot, axis=0) * onehot, axis=1) - 1
    target = (flat_ids * capacity + slot).reshape(tok_rows, 2)
    places = jnp.arange(experts_count * capacity, dtype=jnp.int32)
    spread = (
        (places[:, None] == target[None, :, 0]) | (places[:, None] == target[None, :, 1])
    ).astype(jnp.bfloat16)
    outgoing = (
        jnp.dot(spread, normed, preferred_element_type=jnp.float32)
        .astype(jnp.bfloat16)
        .reshape(experts_count, capacity, normed.shape[1])
    )
    raw_weights = route_weights.astype(jnp.float32)
    share = raw_weights / jnp.sum(raw_weights, axis=1, keepdims=True)
    full_rows = lax.all_gather(
        lax.all_to_all(outgoing, "ctx", split_axis=0, concat_axis=0, tiled=True),
        "head",
        axis=2,
        tiled=True,
    )
    flat = full_rows.reshape(-1, full_rows.shape[2])
    gate = jnp.dot(flat, gate_weight[0], preferred_element_type=jnp.float32)
    up = jnp.dot(flat, up_weight[0], preferred_element_type=jnp.float32)
    gated = (jax.nn.silu(gate) * up).astype(jnp.bfloat16)
    partial_value = jnp.dot(gated, down_weight[0], preferred_element_type=jnp.float32).astype(
        jnp.bfloat16
    )
    summed = lax.psum_scatter(partial_value, "head", scatter_dimension=1, tiled=True)
    answer = summed.reshape(full_rows.shape[0], full_rows.shape[1], summed.shape[1])
    returned = lax.all_to_all(answer, "ctx", split_axis=0, concat_axis=0, tiled=True)
    returned = returned.reshape(-1, returned.shape[2])
    moe = 0.0
    for k in range(2):
        pick = (target[:, k : k + 1] == places[None, :]).astype(jnp.bfloat16)
        moe = moe + share[:, k : k + 1] * jnp.dot(
            pick, returned, preferred_element_type=jnp.float32
        )
    return (hidden_slice + moe).astype(jnp.bfloat16)


def solution(mesh):
    placed = (
        P("ctx", "head"),
        P("ctx", "head"),
        P("ctx", "head"),
        P(),
        P("head"),
        P("head", "ctx"),
        P("ctx", "head"),
        P("head"),
        P("ctx", None),
        P("ctx", None),
        P("ctx", None, "head"),
        P("ctx", None, "head"),
        P("ctx", "head", None),
    )
    return jax.shard_map(
        on_device, mesh=mesh, in_specs=placed, out_specs=P("ctx", "head"), check_vma=False
    )
```

```python
import functools

import jax
import jax.numpy as jnp
from jax import lax
from jax.experimental import pallas as pl
from jax.experimental.pallas import tpu as pltpu
from jax.sharding import PartitionSpec as P

HEAD_DIM = 128


highest = lax.Precision.HIGHEST


MESH = pl.DeviceIdType.MESH


def remote(src, dst, send, recv, ctx, head):
    return pltpu.make_async_remote_copy(
        src_ref=src,
        dst_ref=dst,
        send_sem=send,
        recv_sem=recv,
        device_id=(ctx, head),
        device_id_type=MESH,
    )


def seat():
    head = lax.axis_index("head")
    return lax.axis_index("ctx"), lax.div(head, 2), lax.rem(head, 2)


def greet(ctx_count, chips, across_ctx):
    me, chip, core = seat()
    barrier = pltpu.get_barrier_semaphore()

    def tell(ctx, head):
        pl.semaphore_signal(barrier, inc=1, device_id=(ctx, head), device_id_type=MESH)

    tell(me, chip * 2 + 1 - core)
    for j in range(1, chips):
        tell(me, lax.rem(chip + j, chips) * 2 + core)
    count = chips
    if across_ctx:

        @pl.loop(1, ctx_count)
        def _(i):
            tell(lax.rem(me + i, ctx_count), chip * 2 + core)

        count += ctx_count - 1
    pl.semaphore_wait(barrier, count)


def dispatch_kernel(
    n, chips, out_ref, full_ref, here, a_s, a_r, p_s, p_r, x_s, x_r, f_s, f_r
):
    me, chip, core = seat()
    width = out_ref.shape[2]
    mine, partner = chip * 2 + core, chip * 2 + 1 - core

    def cell(block, head):
        return full_ref.at[block, :, pl.ds(pl.multiple_of(head * width, 128), width)]

    greet(n, chips, True)
    own = pltpu.make_async_copy(out_ref.at[me], cell(me, mine), here)
    own.start()

    def sent(i):
        to = lax.rem(me + i, n)
        return remote(out_ref.at[to], cell(me, mine), a_s.at[i], a_r.at[i], to, mine)

    @pl.loop(1, n)
    def _(i):
        sent(i).start()

    def block_of(i):
        return lax.rem(me - i + n, n)

    def arrived(i):
        return remote(out_ref.at[me], cell(block_of(i), mine), a_s.at[i], a_r.at[i], me, mine)

    def to_partner(i, head):
        b = cell(block_of(i), head)
        return remote(b, b, p_s.at[i], p_r.at[i], me, partner)

    def to_chip(i, j):
        b = cell(block_of(i), mine)
        return remote(b, b, x_s.at[j, i], x_r.at[j, i], me, lax.rem(chip + j, chips) * 2 + core)

    def from_chip(i, j):
        b = cell(block_of(i), lax.rem(chip - j + chips, chips) * 2 + core)
        return remote(b, b, x_s.at[j, i], x_r.at[j, i], me, mine)

    def forward(i, j, which):
        b = cell(block_of(i), lax.rem(chip - j + chips, chips) * 2 + which)
        return remote(b, b, f_s.at[j, i], f_r.at[j, i], me, partner)

    def spread(i):
        for j in range(1, chips):
            to_chip(i, j).start()
        to_partner(i, mine).start()

    def relay(i):
        for j in range(1, chips):
            from_chip(i, j).wait_recv()
            forward(i, j, core).start()

    own.wait()
    spread(0)

    @pl.loop(1, n)
    def _(i):
        arrived(i).wait_recv()
        spread(i)

        @pl.when(i >= 2)
        def _():
            relay(i - 2)

    relay(n - 2)
    relay(n - 1)

    @pl.loop(0, n)
    def _(i):
        to_partner(i, partner).wait_recv()
        to_partner(i, mine).wait_send()
        for j in range(1, chips):
            forward(i, j, 1 - core).wait_recv()
            forward(i, j, core).wait_send()
            to_chip(i, j).wait_send()

    @pl.loop(1, n)
    def _(i):
        sent(i).wait_send()


def dispatch(outgoing, n, heads):
    chips = heads // 2
    rows, width = outgoing.shape[1:]
    dma = pltpu.SemaphoreType.DMA
    return pl.pallas_call(
        functools.partial(dispatch_kernel, n, chips),
        out_shape=jax.ShapeDtypeStruct((n, rows, width * heads), outgoing.dtype),
        in_specs=[pl.BlockSpec(memory_space=pl.ANY)],
        out_specs=pl.BlockSpec(memory_space=pl.ANY),
        scratch_shapes=[dma, dma((n,)), dma((n,)), dma((n,)), dma((n,))]
        + [dma((chips, n))] * 4,
        compiler_params=pltpu.CompilerParams(collective_id=0, has_side_effects=True),
        name="dispatch",
    )(outgoing)


def giveback_kernel(
    n, chips, part_ref, ret_ref, own, pair, out_x, in_x, total, here, l_s, p_s, p_r, x_s, x_r, a_s, a_r
):
    me, chip, core = seat()
    rows, width = ret_ref.shape[1:]
    mine, partner = chip * 2 + core, chip * 2 + 1 - core

    def cell(block, head):
        return part_ref.at[block, :, pl.ds(pl.multiple_of(head * width, 128), width)]

    def block_of(i):
        return lax.rem(me + 1 + i, n)

    def column(j):
        return lax.rem(chip + j, chips)

    def load(i, j):
        return pltpu.make_async_copy(
            cell(block_of(i), column(j) * 2 + core), own.at[i, j], l_s.at[j, i]
        )

    def swap(i, j):
        return remote(
            cell(block_of(i), column(j) * 2 + 1 - core),
            pair.at[i, j],
            p_s.at[j, i],
            p_r.at[j, i],
            me,
            partner,
        )

    def cross(i, j):
        return remote(
            out_x.at[i, j], in_x.at[i, j], x_s.at[j, i], x_r.at[j, i], me, column(j) * 2 + core
        )

    def home(i):
        return remote(
            total.at[i], ret_ref.at[me], a_s.at[i], a_r.at[i], block_of(i), mine
        )

    greet(n, chips, True)

    @pl.loop(0, n)
    def _(i):
        for j in list(range(1, chips)) + [0]:
            swap(i, j).start()
            load(i, j).start()

    def paired(i, j):
        load(i, j).wait()
        swap(i, j).wait_recv()
        return own[i, j].astype(jnp.float32) + pair[i, j].astype(jnp.float32)

    def first(i):
        for j in range(1, chips):
            out_x[i, j] = paired(i, j).astype(jnp.bfloat16)
            cross(i, j).start()

    def second(i):
        acc = paired(i, 0)
        for j in range(1, chips):
            cross(i, j).wait_recv()
            acc = acc + in_x[i, j].astype(jnp.float32)
        total[i] = acc.astype(jnp.bfloat16)

    first(0)
    first(1)

    @pl.loop(0, n - 1)
    def _(i):
        @pl.when(i + 2 < n)
        def _():
            first(i + 2)

        second(i)
        home(i).start()

    second(n - 1)
    keep = pltpu.make_async_copy(total.at[n - 1], ret_ref.at[me], here)
    keep.start()

    @pl.loop(0, n - 1)
    def _(i):
        back = lax.rem(me - 1 - i + n, n)
        remote(total.at[i], ret_ref.at[back], a_s.at[i], a_r.at[i], me, mine).wait_recv()
        home(i).wait_send()

    @pl.loop(0, n)
    def _(i):
        for j in range(chips):
            swap(i, j).wait_send()
        for j in range(1, chips):
            cross(i, j).wait_send()

    keep.wait()


def giveback(partial_value, n, heads):
    chips = heads // 2
    rows, width = partial_value.shape[1], partial_value.shape[2] // heads
    dma = pltpu.SemaphoreType.DMA
    piece = pltpu.VMEM((n, chips, rows, width), jnp.bfloat16)
    return pl.pallas_call(
        functools.partial(giveback_kernel, n, chips),
        out_shape=jax.ShapeDtypeStruct((n, rows, width), jnp.bfloat16),
        in_specs=[pl.BlockSpec(memory_space=pl.ANY)],
        out_specs=pl.BlockSpec(memory_space=pl.ANY),
        scratch_shapes=[piece, piece, piece, piece, pltpu.VMEM((n, rows, width), jnp.bfloat16)]
        + [dma]
        + [dma((chips, n))] * 5
        + [dma((n,))] * 2,
        compiler_params=pltpu.CompilerParams(collective_id=1, has_side_effects=True),
        name="giveback",
    )(partial_value)


def episode_of(positions, lengths):
    starts = jnp.cumsum(lengths) - lengths
    return jnp.sum((starts[None, :] <= positions[:, None]).astype(jnp.int32), axis=1) - 1


def on_device(
    query,
    key,
    value,
    episode_lengths,
    attn_gain,
    out_weight,
    residual,
    norm_gain,
    expert_ids,
    route_weights,
    gate_weight,
    up_weight,
    down_weight,
):
    tok_rows = query.shape[0]
    head_size = HEAD_DIM
    heads_local = query.shape[1] // head_size
    own_index = lax.axis_index("ctx")
    ctx_count = lax.axis_size("ctx")
    positions = own_index * tok_rows + jnp.arange(tok_rows, dtype=jnp.int32)
    episode = episode_of(positions, episode_lengths)
    prior = episode_of(positions[:1] - 1, episode_lengths)[0]
    final = episode[-1]
    lifted_query = jax.nn.silu(query.astype(jnp.float32)).reshape(tok_rows, heads_local, head_size)
    lifted_key = jax.nn.silu(key.astype(jnp.float32)).reshape(tok_rows, heads_local, head_size)
    value_rows = value.astype(jnp.float32).reshape(tok_rows, heads_local, head_size)
    keep = (episode == final).astype(jnp.float32)
    state = jnp.einsum(
        "shd,she->hde", lifted_key * keep[:, None, None], value_rows, precision=highest
    )
    finals = episode_of(
        (jnp.arange(ctx_count, dtype=jnp.int32) + 1) * tok_rows - 1, episode_lengths
    )
    earlier = (jnp.arange(ctx_count) < own_index) & (finals == prior)
    gathered = lax.all_gather(state.astype(jnp.bfloat16), "ctx")
    carry_state = jnp.sum(
        jnp.where(earlier[:, None, None, None], gathered.astype(jnp.float32), 0.0), axis=0
    )
    order = jnp.arange(tok_rows, dtype=jnp.int32)
    allowed = ((order[:, None] >= order[None, :]) & (episode[:, None] == episode[None, :])).astype(
        jnp.float32
    )
    scores = jnp.einsum("thd,shd->hts", lifted_query, lifted_key, precision=highest)
    inside = jnp.einsum("hts,shd->thd", scores * allowed[None], value_rows, precision=highest)
    outside = jnp.einsum("thd,hde->the", lifted_query, carry_state, precision=highest)
    attn = inside + outside * (episode == prior).astype(jnp.float32)[:, None, None]
    mean_square = jnp.mean(attn * attn, axis=2, keepdims=True)
    scaled = attn * lax.rsqrt(mean_square + 1e-06) * attn_gain.reshape(heads_local, head_size)
    headed = scaled.reshape(tok_rows, heads_local * head_size).astype(jnp.bfloat16)
    mixed_part = jnp.dot(
        headed,
        lax.all_gather(out_weight, "ctx", axis=1, tiled=True),
        preferred_element_type=jnp.float32,
    )
    width = mixed_part.shape[1]
    mixed_slice = lax.psum_scatter(
        mixed_part.astype(jnp.bfloat16), "head", scatter_dimension=1, tiled=True
    ).astype(jnp.float32)
    hidden_slice = residual.astype(jnp.float32) + mixed_slice
    squares = lax.psum(jnp.sum(hidden_slice * hidden_slice, axis=1), "head")
    normed = (hidden_slice * lax.rsqrt(squares / width + 1e-06)[:, None] * norm_gain).astype(
        jnp.bfloat16
    )
    experts_count = gate_weight.shape[0] * ctx_count
    capacity = 3 * tok_rows // experts_count
    flat_ids = expert_ids.reshape(-1)
    onehot = (flat_ids[:, None] == jnp.arange(experts_count, dtype=jnp.int32)[None, :]).astype(
        jnp.int32
    )
    slot = jnp.sum(jnp.cumsum(onehot, axis=0) * onehot, axis=1) - 1
    target = (flat_ids * capacity + slot).reshape(tok_rows, 2)
    places = jnp.arange(experts_count * capacity, dtype=jnp.int32)
    spread = (
        (places[:, None] == target[None, :, 0]) | (places[:, None] == target[None, :, 1])
    ).astype(jnp.bfloat16)
    outgoing = (
        jnp.dot(spread, normed, preferred_element_type=jnp.float32)
        .astype(jnp.bfloat16)
        .reshape(experts_count, capacity, normed.shape[1])
    )
    raw_weights = route_weights.astype(jnp.float32)
    share = raw_weights / jnp.sum(raw_weights, axis=1, keepdims=True)
    full_rows = dispatch(outgoing, ctx_count, lax.axis_size("head"))
    flat = full_rows.reshape(-1, full_rows.shape[2])
    gate = jnp.dot(flat, gate_weight[0], preferred_element_type=jnp.float32)
    up = jnp.dot(flat, up_weight[0], preferred_element_type=jnp.float32)
    gated = (jax.nn.silu(gate) * up).astype(jnp.bfloat16)
    partial_value = jnp.dot(gated, down_weight[0], preferred_element_type=jnp.float32).astype(
        jnp.bfloat16
    )
    returned = giveback(
        partial_value.reshape(full_rows.shape), ctx_count, lax.axis_size("head")
    )
    returned = returned.reshape(-1, returned.shape[2])
    moe = 0.0
    for k in range(2):
        pick = (target[:, k : k + 1] == places[None, :]).astype(jnp.bfloat16)
        moe = moe + share[:, k : k + 1] * jnp.dot(
            pick, returned, preferred_element_type=jnp.float32
        )
    return (hidden_slice + moe).astype(jnp.bfloat16)


def solution(mesh):
    placed = (
        P("ctx", "head"),
        P("ctx", "head"),
        P("ctx", "head"),
        P(),
        P("head"),
        P("head", "ctx"),
        P("ctx", "head"),
        P("head"),
        P("ctx", None),
        P("ctx", None),
        P("ctx", None, "head"),
        P("ctx", None, "head"),
        P("ctx", "head", None),
    )
    return jax.shard_map(
        on_device, mesh=mesh, in_specs=placed, out_specs=P("ctx", "head"), check_vma=False
    )
```

```python
import functools

import jax
import jax.numpy as jnp
from jax import lax
from jax.experimental import pallas as pl
from jax.experimental.pallas import tpu as pltpu
from jax.sharding import PartitionSpec as P

HEAD_DIM = 128


highest = lax.Precision.HIGHEST


MESH = pl.DeviceIdType.MESH


def remote(src, dst, send, recv, ctx, head):
    return pltpu.make_async_remote_copy(
        src_ref=src,
        dst_ref=dst,
        send_sem=send,
        recv_sem=recv,
        device_id=(ctx, head),
        device_id_type=MESH,
    )


def seat():
    head = lax.axis_index("head")
    return lax.axis_index("ctx"), lax.div(head, 2), lax.rem(head, 2)


def greet(ctx_count, chips, across_ctx):
    me, chip, core = seat()
    barrier = pltpu.get_barrier_semaphore()

    def tell(ctx, head):
        pl.semaphore_signal(barrier, inc=1, device_id=(ctx, head), device_id_type=MESH)

    tell(me, chip * 2 + 1 - core)
    for j in range(1, chips):
        tell(me, lax.rem(chip + j, chips) * 2 + core)
    count = chips
    if across_ctx:

        @pl.loop(1, ctx_count)
        def _(i):
            tell(lax.rem(me + i, ctx_count), chip * 2 + core)

        count += ctx_count - 1
    pl.semaphore_wait(barrier, count)


def dispatch_kernel(
    n, chips, out_ref, full_ref, here, a_s, a_r, p_s, p_r, x_s, x_r, f_s, f_r
):
    me, chip, core = seat()
    width = out_ref.shape[2]
    mine, partner = chip * 2 + core, chip * 2 + 1 - core

    def cell(block, head):
        return full_ref.at[block, :, pl.ds(pl.multiple_of(head * width, 128), width)]

    greet(n, chips, True)
    own = pltpu.make_async_copy(out_ref.at[me], cell(me, mine), here)
    own.start()

    def sent(i):
        to = lax.rem(me + i, n)
        return remote(out_ref.at[to], cell(me, mine), a_s.at[i], a_r.at[i], to, mine)

    @pl.loop(1, n)
    def _(i):
        sent(i).start()

    def block_of(i):
        return lax.rem(me - i + n, n)

    def arrived(i):
        return remote(out_ref.at[me], cell(block_of(i), mine), a_s.at[i], a_r.at[i], me, mine)

    def to_partner(i, head):
        b = cell(block_of(i), head)
        return remote(b, b, p_s.at[i], p_r.at[i], me, partner)

    def to_chip(i, j):
        b = cell(block_of(i), mine)
        return remote(b, b, x_s.at[j, i], x_r.at[j, i], me, lax.rem(chip + j, chips) * 2 + core)

    def from_chip(i, j):
        b = cell(block_of(i), lax.rem(chip - j + chips, chips) * 2 + core)
        return remote(b, b, x_s.at[j, i], x_r.at[j, i], me, mine)

    def forward(i, j, which):
        b = cell(block_of(i), lax.rem(chip - j + chips, chips) * 2 + which)
        return remote(b, b, f_s.at[j, i], f_r.at[j, i], me, partner)

    def spread(i):
        for j in range(1, chips):
            to_chip(i, j).start()
        to_partner(i, mine).start()

    def relay(i):
        for j in range(1, chips):
            from_chip(i, j).wait_recv()
            forward(i, j, core).start()

    own.wait()
    spread(0)

    @pl.loop(1, n)
    def _(i):
        arrived(i).wait_recv()
        spread(i)

        @pl.when(i >= 2)
        def _():
            relay(i - 2)

    relay(n - 2)
    relay(n - 1)

    @pl.loop(0, n)
    def _(i):
        to_partner(i, partner).wait_recv()
        to_partner(i, mine).wait_send()
        for j in range(1, chips):
            forward(i, j, 1 - core).wait_recv()
            forward(i, j, core).wait_send()
            to_chip(i, j).wait_send()

    @pl.loop(1, n)
    def _(i):
        sent(i).wait_send()


def dispatch(outgoing, n, heads):
    chips = heads // 2
    rows, width = outgoing.shape[1:]
    dma = pltpu.SemaphoreType.DMA
    return pl.pallas_call(
        functools.partial(dispatch_kernel, n, chips),
        out_shape=jax.ShapeDtypeStruct((n, rows, width * heads), outgoing.dtype),
        in_specs=[pl.BlockSpec(memory_space=pl.ANY)],
        out_specs=pl.BlockSpec(memory_space=pl.ANY),
        scratch_shapes=[dma, dma((n,)), dma((n,)), dma((n,)), dma((n,))]
        + [dma((chips, n))] * 4,
        compiler_params=pltpu.CompilerParams(collective_id=0, has_side_effects=True),
        name="dispatch",
    )(outgoing)


def giveback_kernel(
    n, chips, part_ref, ret_ref, own, pair, out_x, in_x, total, here, l_s, p_s, p_r, x_s, x_r, a_s, a_r
):
    me, chip, core = seat()
    rows, width = ret_ref.shape[1:]
    mine, partner = chip * 2 + core, chip * 2 + 1 - core

    def cell(block, head):
        return part_ref.at[block, :, pl.ds(pl.multiple_of(head * width, 128), width)]

    def block_of(i):
        return lax.rem(me + 1 + i, n)

    def column(j):
        return lax.rem(chip + j, chips)

    def load(i, j):
        return pltpu.make_async_copy(
            cell(block_of(i), column(j) * 2 + core), own.at[i, j], l_s.at[j, i]
        )

    def swap(i, j):
        return remote(
            cell(block_of(i), column(j) * 2 + 1 - core),
            pair.at[i, j],
            p_s.at[j, i],
            p_r.at[j, i],
            me,
            partner,
        )

    def cross(i, j):
        return remote(
            out_x.at[i, j], in_x.at[i, j], x_s.at[j, i], x_r.at[j, i], me, column(j) * 2 + core
        )

    def home(i):
        return remote(
            total.at[i], ret_ref.at[me], a_s.at[i], a_r.at[i], block_of(i), mine
        )

    greet(n, chips, True)

    @pl.loop(0, n)
    def _(i):
        for j in list(range(1, chips)) + [0]:
            swap(i, j).start()
            load(i, j).start()

    def paired(i, j):
        load(i, j).wait()
        swap(i, j).wait_recv()
        return own[i, j].astype(jnp.float32) + pair[i, j].astype(jnp.float32)

    def first(i):
        for j in range(1, chips):
            out_x[i, j] = paired(i, j).astype(jnp.bfloat16)
            cross(i, j).start()

    def second(i):
        acc = paired(i, 0)
        for j in range(1, chips):
            cross(i, j).wait_recv()
            acc = acc + in_x[i, j].astype(jnp.float32)
        total[i] = acc.astype(jnp.bfloat16)

    first(0)
    first(1)

    @pl.loop(0, n - 1)
    def _(i):
        @pl.when(i + 2 < n)
        def _():
            first(i + 2)

        second(i)
        home(i).start()

    second(n - 1)
    keep = pltpu.make_async_copy(total.at[n - 1], ret_ref.at[me], here)
    keep.start()

    @pl.loop(0, n - 1)
    def _(i):
        back = lax.rem(me - 1 - i + n, n)
        remote(total.at[i], ret_ref.at[back], a_s.at[i], a_r.at[i], me, mine).wait_recv()
        home(i).wait_send()

    @pl.loop(0, n)
    def _(i):
        for j in range(chips):
            swap(i, j).wait_send()
        for j in range(1, chips):
            cross(i, j).wait_send()

    keep.wait()


def giveback(partial_value, n, heads):
    chips = heads // 2
    rows, width = partial_value.shape[1], partial_value.shape[2] // heads
    dma = pltpu.SemaphoreType.DMA
    piece = pltpu.VMEM((n, chips, rows, width), jnp.bfloat16)
    return pl.pallas_call(
        functools.partial(giveback_kernel, n, chips),
        out_shape=jax.ShapeDtypeStruct((n, rows, width), jnp.bfloat16),
        in_specs=[pl.BlockSpec(memory_space=pl.ANY)],
        out_specs=pl.BlockSpec(memory_space=pl.ANY),
        scratch_shapes=[piece, piece, piece, piece, pltpu.VMEM((n, rows, width), jnp.bfloat16)]
        + [dma]
        + [dma((chips, n))] * 5
        + [dma((n,))] * 2,
        compiler_params=pltpu.CompilerParams(collective_id=1, has_side_effects=True),
        name="giveback",
    )(partial_value)


def attend_kernel(
    n,
    heads,
    q_ref,
    k_ref,
    v_ref,
    allowed_ref,
    keep_ref,
    carry_ref,
    earlier_ref,
    gain_ref,
    w_ref,
    res_ref,
    hidden_ref,
    squares_ref,
    wall,
    states,
    attn,
    headed,
    acc,
    mixed,
    pair,
    out_x,
    in_x,
    sq_own,
    sq_all,
    here,
    w_s,
    w_r,
    s_s,
    s_r,
    p_s,
    p_r,
    x_s,
    x_r,
    q_s,
    q_r,
):
    me, chip, core = seat()
    chips = heads // 2
    mine, partner = chip * 2 + core, chip * 2 + 1 - core
    local, size = states.shape[1], HEAD_DIM
    half, piece = w_ref.shape[0] // 2, w_ref.shape[0] // 4
    group = n // heads
    f32 = jnp.float32

    def seat_at(p):
        return 2 * p - lax.div(p, n // 2) * (4 * p - 2 * n + 1)

    low = lax.div(me, 2)
    place = low + lax.rem(me, 2) * (n - lax.div(me + 1, 2) - low)
    ahead = [seat_at(lax.rem(place + 1, n)), seat_at(lax.rem(place + n - 1, n))]

    def origin(way, distance):
        step = n - distance if way == 0 else distance
        return seat_at(lax.rem(place + step, n))

    barrier = pltpu.get_barrier_semaphore()

    def tell(ctx, head):
        pl.semaphore_signal(barrier, inc=1, device_id=(ctx, head), device_id_type=MESH)

    tell(ahead[0], mine)
    tell(ahead[1], mine)
    for j in range(1, heads):
        tell(me, lax.rem(mine + j, heads))
    pl.semaphore_wait(barrier, heads + 1)

    def w_rows(way, part):
        return pl.ds(way * half + part * piece, piece)

    def w_first(way, part):
        rows = w_rows(way, part)
        return remote(
            w_ref.at[rows],
            wall.at[me, rows],
            w_s.at[way, part, 0],
            w_r.at[way, part, 0],
            ahead[way],
            mine,
        )

    def w_step(way, part, held, stage):
        cell = wall.at[origin(way, held), w_rows(way, part)]
        return remote(
            cell, cell, w_s.at[way, part, stage], w_r.at[way, part, stage], ahead[way], mine
        )

    def s_step(way, held, stage):
        cell = states.at[origin(way, held), pl.ds(way * (local // 2), local // 2)]
        return remote(cell, cell, s_s.at[way, stage], s_r.at[way, stage], ahead[way], mine)

    for part in range(2):
        for way in range(2):
            w_first(way, part).start()
    own = pltpu.make_async_copy(w_ref, wall.at[me], here)
    own.start()

    def columns(h):
        return pl.ds(pl.multiple_of(h * size, size), size)

    def lifted(ref, h):
        x = ref[:, columns(h)].astype(f32)
        return x / (1.0 + jnp.exp(-x))

    @pl.loop(0, local)
    def _(h):
        kept = lifted(k_ref, h) * keep_ref[...]
        state = jnp.dot(
            kept.T, v_ref[:, columns(h)].astype(f32), precision=highest, preferred_element_type=f32
        )
        states[me, h] = state.astype(jnp.bfloat16)

    for way in range(2):
        s_step(way, 0, 0).start()

    @pl.loop(0, local)
    def _(h):
        scores = lax.dot_general(
            lifted(q_ref, h),
            lifted(k_ref, h),
            (((1,), (1,)), ((), ())),
            precision=highest,
            preferred_element_type=f32,
        )
        attn[:, columns(h)] = jnp.dot(
            scores * allowed_ref[...],
            v_ref[:, columns(h)].astype(f32),
            precision=highest,
            preferred_element_type=f32,
        )

    acc[...] = jnp.zeros_like(acc)

    def s_stage(stage):
        for way in range(2):
            s_step(way, stage + 1, stage).wait_recv()

            @pl.when(stage < n - 2)
            def _():
                s_step(way, stage + 1, stage + 1).start()

    def w_stage(stage):
        for part in range(2):
            for way in range(2):
                w_step(way, part, stage + 1, stage).wait_recv()

                @pl.when(stage < n - 2)
                def _():
                    w_step(way, part, stage + 1, stage + 1).start()

    early = (n - 2) // 2

    @pl.loop(0, early)
    def _(t):
        s_stage(2 * t)
        s_stage(2 * t + 1)
        w_stage(t)

    s_stage(n - 2)

    @pl.loop(0, local)
    def _(h):
        def add(j, total):
            return total + earlier_ref[j] * states[j, h].astype(f32)

        state = lax.fori_loop(0, n, add, jnp.zeros((size, size), f32))
        outside = jnp.dot(
            lifted(q_ref, h), state, precision=highest, preferred_element_type=f32
        )
        full = attn[:, columns(h)] + outside * carry_ref[...]
        mean_square = jnp.mean(full * full, axis=1, keepdims=True)
        scaled = full * lax.rsqrt(mean_square + 1e-06) * gain_ref[:, columns(h)]
        headed[:, columns(h)] = scaled.astype(jnp.bfloat16)

    def project(way, held):
        src = origin(way, held)
        rows = pl.ds(way * half, half)
        acc[src] += jnp.dot(headed[:, rows], wall[src, rows], preferred_element_type=f32)

    own.wait()

    @pl.loop(0, early + 1)
    def _(held):
        project(0, held)
        project(1, held)

    @pl.loop(early, n - 1)
    def _(stage):
        w_stage(stage)
        project(0, stage + 1)
        project(1, stage + 1)

    mixed[...] = acc[...].astype(jnp.bfloat16)

    def column(j):
        return lax.rem(chip + j, chips)

    def blocks(head):
        return pl.ds(head * group, group)

    def swap(j):
        return remote(
            mixed.at[blocks(column(j) * 2 + 1 - core)],
            pair.at[j],
            p_s.at[j],
            p_r.at[j],
            me,
            partner,
        )

    def cross(j):
        return remote(
            out_x.at[j], in_x.at[j], x_s.at[j], x_r.at[j], me, column(j) * 2 + core
        )

    for j in list(range(1, chips)) + [0]:
        swap(j).start()

    def paired(j):
        swap(j).wait_recv()
        return acc[blocks(column(j) * 2 + core)] + pair[j].astype(f32)

    for j in range(1, chips):
        out_x[j] = paired(j).astype(jnp.bfloat16)
        cross(j).start()
    total = paired(0) + res_ref[...].astype(f32)
    hidden_ref[...] = total
    for j in range(1, chips):
        cross(j).wait_recv()
        hidden_ref[...] += in_x[j].astype(f32)
    ones = jnp.ones((8, hidden_ref.shape[2]), f32)
    squares = jnp.zeros((8, hidden_ref.shape[1]), f32)
    for b in range(group):
        part = hidden_ref[b]
        squares = squares + lax.dot_general(
            ones,
            part * part,
            (((1,), (1,)), ((), ())),
            precision=highest,
            preferred_element_type=f32,
        )
    sq_own[...] = squares

    def share(j, to, slot):
        return remote(sq_own, sq_all.at[slot], q_s.at[j], q_r.at[j], me, to)

    for j in range(1, heads):
        share(j, lax.rem(mine + j, heads), j).start()
    for j in range(1, heads):
        share(j, mine, j).wait_recv()
        squares = squares + sq_all[j]
    squares_ref[...] = squares

    for j in range(1, heads):
        share(j, mine, j).wait_send()
    for j in range(chips):
        swap(j).wait_send()
    for j in range(1, chips):
        cross(j).wait_send()

    for part in range(2):
        for way in range(2):
            w_first(way, part).wait_send()

    @pl.loop(0, n - 1)
    def _(stage):
        for way in range(2):
            s_step(way, stage, stage).wait_send()

    @pl.loop(1, n - 1)
    def _(stage):
        for part in range(2):
            for way in range(2):
                w_step(way, part, stage, stage).wait_send()


def attend(query, key, value, allowed, keep, carry, earlier, gain, weight, residual, n, heads):
    rows, feats = query.shape
    width, group = weight.shape[1], n // heads
    local, chips = feats // HEAD_DIM, heads // 2
    dma = pltpu.SemaphoreType.DMA
    bf16, f32 = jnp.bfloat16, jnp.float32
    vmem = pl.BlockSpec(memory_space=pltpu.VMEM)
    piece = pltpu.VMEM((chips, group, rows, width), bf16)
    return pl.pallas_call(
        functools.partial(attend_kernel, n, heads),
        out_shape=(
            jax.ShapeDtypeStruct((group, rows, width), f32),
            jax.ShapeDtypeStruct((8, rows), f32),
        ),
        in_specs=[vmem] * 8 + [pl.BlockSpec(memory_space=pl.ANY), vmem],
        out_specs=(vmem, vmem),
        scratch_shapes=[
            pltpu.VMEM((n,) + weight.shape, bf16),
            pltpu.VMEM((n, local, HEAD_DIM, HEAD_DIM), bf16),
            pltpu.VMEM((rows, feats), f32),
            pltpu.VMEM((rows, feats), bf16),
            pltpu.VMEM((n, rows, width), f32),
            pltpu.VMEM((n, rows, width), bf16),
            piece,
            piece,
            piece,
            pltpu.VMEM((8, rows), f32),
            pltpu.VMEM((heads, 8, rows), f32),
            dma,
            dma((2, 2, n)),
            dma((2, 2, n)),
            dma((2, n)),
            dma((2, n)),
            dma((chips,)),
            dma((chips,)),
            dma((chips,)),
            dma((chips,)),
            dma((heads,)),
            dma((heads,)),
        ],
        compiler_params=pltpu.CompilerParams(
            collective_id=2, has_side_effects=True, vmem_limit_bytes=60 * 1024 * 1024
        ),
        name="attend",
    )(query, key, value, allowed, keep, carry, earlier, gain, weight, residual)


def episode_of(positions, lengths):
    starts = jnp.cumsum(lengths) - lengths
    return jnp.sum((starts[None, :] <= positions[:, None]).astype(jnp.int32), axis=1) - 1


def on_device(
    query,
    key,
    value,
    episode_lengths,
    attn_gain,
    out_weight,
    residual,
    norm_gain,
    expert_ids,
    route_weights,
    gate_weight,
    up_weight,
    down_weight,
):
    tok_rows = query.shape[0]
    head_size = HEAD_DIM
    own_index = lax.axis_index("ctx")
    ctx_count = lax.axis_size("ctx")
    positions = own_index * tok_rows + jnp.arange(tok_rows, dtype=jnp.int32)
    episode = episode_of(positions, episode_lengths)
    prior = episode_of(positions[:1] - 1, episode_lengths)[0]
    final = episode[-1]
    keep = (episode == final).astype(jnp.float32)
    finals = episode_of(
        (jnp.arange(ctx_count, dtype=jnp.int32) + 1) * tok_rows - 1, episode_lengths
    )
    earlier = (jnp.arange(ctx_count) < own_index) & (finals == prior)
    earlier = jnp.broadcast_to(
        earlier.astype(jnp.float32)[:, None, None], (ctx_count, 1, head_size)
    )
    order = jnp.arange(tok_rows, dtype=jnp.int32)
    allowed = ((order[:, None] >= order[None, :]) & (episode[:, None] == episode[None, :])).astype(
        jnp.float32
    )
    heads = lax.axis_size("head")
    col = out_weight.shape[1]
    width = residual.shape[1] * heads
    hidden_blocks, squares = attend(
        query,
        key,
        value,
        allowed,
        keep[:, None],
        (episode == prior).astype(jnp.float32)[:, None],
        earlier,
        attn_gain[None, :],
        out_weight,
        jnp.swapaxes(residual.reshape(tok_rows, -1, col), 0, 1),
        ctx_count,
        heads,
    )
    hidden_slice = jnp.swapaxes(hidden_blocks, 0, 1).reshape(tok_rows, -1)
    normed = (
        hidden_slice * lax.rsqrt(squares[0] / width + 1e-06)[:, None] * norm_gain
    ).astype(jnp.bfloat16)
    experts_count = gate_weight.shape[0] * ctx_count
    capacity = 3 * tok_rows // experts_count
    flat_ids = expert_ids.reshape(-1)
    onehot = (flat_ids[:, None] == jnp.arange(experts_count, dtype=jnp.int32)[None, :]).astype(
        jnp.int32
    )
    slot = jnp.sum(jnp.cumsum(onehot, axis=0) * onehot, axis=1) - 1
    target = (flat_ids * capacity + slot).reshape(tok_rows, 2)
    places = jnp.arange(experts_count * capacity, dtype=jnp.int32)
    spread = (
        (places[:, None] == target[None, :, 0]) | (places[:, None] == target[None, :, 1])
    ).astype(jnp.bfloat16)
    outgoing = (
        jnp.dot(spread, normed, preferred_element_type=jnp.float32)
        .astype(jnp.bfloat16)
        .reshape(experts_count, capacity, normed.shape[1])
    )
    raw_weights = route_weights.astype(jnp.float32)
    share = raw_weights / jnp.sum(raw_weights, axis=1, keepdims=True)
    full_rows = dispatch(outgoing, ctx_count, lax.axis_size("head"))
    flat = full_rows.reshape(-1, full_rows.shape[2])
    gate = jnp.dot(flat, gate_weight[0], preferred_element_type=jnp.float32)
    up = jnp.dot(flat, up_weight[0], preferred_element_type=jnp.float32)
    gated = (jax.nn.silu(gate) * up).astype(jnp.bfloat16)
    partial_value = jnp.dot(gated, down_weight[0], preferred_element_type=jnp.float32).astype(
        jnp.bfloat16
    )
    returned = giveback(
        partial_value.reshape(full_rows.shape), ctx_count, lax.axis_size("head")
    )
    returned = returned.reshape(-1, returned.shape[2])
    moe = 0.0
    for k in range(2):
        pick = (target[:, k : k + 1] == places[None, :]).astype(jnp.bfloat16)
        moe = moe + share[:, k : k + 1] * jnp.dot(
            pick, returned, preferred_element_type=jnp.float32
        )
    return (hidden_slice + moe).astype(jnp.bfloat16)


def solution(mesh):
    placed = (
        P("ctx", "head"),
        P("ctx", "head"),
        P("ctx", "head"),
        P(),
        P("head"),
        P("head", "ctx"),
        P("ctx", "head"),
        P("head"),
        P("ctx", None),
        P("ctx", None),
        P("ctx", None, "head"),
        P("ctx", None, "head"),
        P("ctx", "head", None),
    )
    return jax.shard_map(
        on_device, mesh=mesh, in_specs=placed, out_specs=P("ctx", "head"), check_vma=False
    )
```

```python
import functools

import jax
import jax.numpy as jnp
from jax import lax
from jax.experimental import pallas as pl
from jax.experimental.pallas import tpu as pltpu
from jax.sharding import PartitionSpec as P

HEAD_DIM = 128


highest = lax.Precision.HIGHEST


MESH = pl.DeviceIdType.MESH


def remote(src, dst, send, recv, ctx, head):
    return pltpu.make_async_remote_copy(
        src_ref=src,
        dst_ref=dst,
        send_sem=send,
        recv_sem=recv,
        device_id=(ctx, head),
        device_id_type=MESH,
    )


def seat():
    head = lax.axis_index("head")
    return lax.axis_index("ctx"), lax.div(head, 2), lax.rem(head, 2)


def greet(ctx_count, chips, across_ctx):
    me, chip, core = seat()
    barrier = pltpu.get_barrier_semaphore()

    def tell(ctx, head):
        pl.semaphore_signal(barrier, inc=1, device_id=(ctx, head), device_id_type=MESH)

    tell(me, chip * 2 + 1 - core)
    for j in range(1, chips):
        tell(me, lax.rem(chip + j, chips) * 2 + core)
    count = chips
    if across_ctx:

        @pl.loop(1, ctx_count)
        def _(i):
            tell(lax.rem(me + i, ctx_count), chip * 2 + core)

        count += ctx_count - 1
    pl.semaphore_wait(barrier, count)


def dispatch_kernel(
    n,
    chips,
    pair,
    out_ref,
    gate_ref,
    up_ref,
    gated_ref,
    full_ref,
    gate_w,
    up_w,
    here,
    w_s,
    a_s,
    a_r,
    p_s,
    p_r,
    x_s,
    x_r,
    f_s,
    f_r,
):
    me, chip, core = seat()
    width = out_ref.shape[2]
    mine, partner = chip * 2 + core, chip * 2 + 1 - core

    def cell(block, head):
        return full_ref.at[block, :, pl.ds(pl.multiple_of(head * width, 128), width)]

    greet(n, chips, True)
    own = pltpu.make_async_copy(out_ref.at[me], cell(0, mine), here)
    own.start()
    weights = [
        pltpu.make_async_copy(gate_ref, gate_w, w_s.at[0]),
        pltpu.make_async_copy(up_ref, up_w, w_s.at[1]),
    ]

    def sent(i):
        to = lax.rem(me + i, n)
        return remote(out_ref.at[to], cell(i, mine), a_s.at[i], a_r.at[i], to, mine)

    @pl.loop(1, n)
    def _(i):
        sent(i).start()

    for copy in weights:
        copy.start()

    def arrived(i):
        return remote(out_ref.at[me], cell(i, mine), a_s.at[i], a_r.at[i], me, mine)

    def to_partner(i, head):
        b = cell(i, head)
        return remote(b, b, p_s.at[i], p_r.at[i], me, partner)

    def to_chip(i, j):
        b = cell(i, mine)
        return remote(b, b, x_s.at[j, i], x_r.at[j, i], me, lax.rem(chip + j, chips) * 2 + core)

    def from_chip(i, j):
        b = cell(i, lax.rem(chip - j + chips, chips) * 2 + core)
        return remote(b, b, x_s.at[j, i], x_r.at[j, i], me, mine)

    def forward(i, j, which):
        b = cell(i, lax.rem(chip - j + chips, chips) * 2 + which)
        return remote(b, b, f_s.at[j, i], f_r.at[j, i], me, partner)

    def spread(i):
        for j in range(1, chips):
            to_chip(i, j).start()
        to_partner(i, mine).start()

    def relay(i):
        for j in range(1, chips):
            from_chip(i, j).wait_recv()
            forward(i, j, core).start()

    def multiply(slot):
        rows = full_ref[pl.ds(slot, pair)]
        rows = rows.reshape(pair * rows.shape[1], rows.shape[2])
        columns = gate_w.shape[1]
        tile = 640 if columns % 640 == 0 else columns
        for start in range(0, columns, tile):
            part = slice(start, start + tile)
            gate = jnp.dot(rows, gate_w[:, part], preferred_element_type=jnp.float32)
            up = jnp.dot(rows, up_w[:, part], preferred_element_type=jnp.float32)
            gated = (gate / (1.0 + jnp.exp(-gate)) * up).astype(jnp.bfloat16)
            gated_ref[pl.ds(slot, pair), :, part] = gated.reshape(pair, -1, tile)

    def complete(slot):
        for e in range(pair):
            to_partner(slot + e, partner).wait_recv()
            for j in range(1, chips):
                forward(slot + e, j, 1 - core).wait_recv()

    own.wait()
    spread(0)

    @pl.loop(1, n)
    def _(i):
        arrived(i).wait_recv()
        spread(i)

        @pl.when(i >= 2)
        def _():
            relay(i - 2)

        @pl.when(i == 4)
        def _():
            for copy in weights:
                copy.wait()

        @pl.when((i >= 3 + pair) & (lax.rem(i, pair) == pair - 1))
        def _():
            complete(i - 3 - pair)
            multiply(i - 3 - pair)

    relay(n - 2)
    relay(n - 1)

    @pl.loop(0, 4 // pair)
    def _(t):
        complete(n - 4 + t * pair)
        multiply(n - 4 + t * pair)

    @pl.loop(0, n)
    def _(i):
        to_partner(i, mine).wait_send()
        for j in range(1, chips):
            forward(i, j, core).wait_send()
            to_chip(i, j).wait_send()

    @pl.loop(1, n)
    def _(i):
        sent(i).wait_send()


def dispatch(outgoing, gate, up, n, heads):
    chips = heads // 2
    rows, width = outgoing.shape[1:]
    dma = pltpu.SemaphoreType.DMA
    return pl.pallas_call(
        functools.partial(dispatch_kernel, n, chips, 2 if rows % 16 == 0 else 1),
        out_shape=jax.ShapeDtypeStruct((n, rows, gate.shape[1]), outgoing.dtype),
        in_specs=[pl.BlockSpec(memory_space=pl.ANY)] * 3,
        out_specs=pl.BlockSpec(memory_space=pltpu.VMEM),
        scratch_shapes=[
            pltpu.VMEM((n, rows, width * heads), outgoing.dtype),
            pltpu.VMEM(gate.shape, gate.dtype),
            pltpu.VMEM(up.shape, up.dtype),
        ]
        + [dma, dma((2,)), dma((n,)), dma((n,)), dma((n,)), dma((n,))]
        + [dma((chips, n))] * 4,
        compiler_params=pltpu.CompilerParams(
            collective_id=0, has_side_effects=True, vmem_limit_bytes=60 * 1024 * 1024
        ),
        name="dispatch",
    )(outgoing, gate, up)


def giveback_kernel(
    n, chips, batch, gated_ref, down_ref, ret_ref, part_ref, pair, out_x, in_x, total, here, p_s, p_r, x_s, x_r, a_s, a_r
):
    me, chip, core = seat()
    rows, width = ret_ref.shape[1:]
    mine, partner = chip * 2 + core, chip * 2 + 1 - core

    def cell(block, head):
        return part_ref.at[block, :, pl.ds(pl.multiple_of(head * width, 128), width)]

    def block_of(i):
        return lax.rem(me + 1 + i, n)

    def column(j):
        return lax.rem(chip + j, chips)

    def swap(i, j):
        return remote(
            cell(n - 1 - i, column(j) * 2 + 1 - core),
            pair.at[i, j],
            p_s.at[j, i],
            p_r.at[j, i],
            me,
            partner,
        )

    def cross(i, j):
        return remote(
            out_x.at[i, j], in_x.at[i, j], x_s.at[j, i], x_r.at[j, i], me, column(j) * 2 + core
        )

    def home(i):
        return remote(
            total.at[i], ret_ref.at[me], a_s.at[i], a_r.at[i], block_of(i), mine
        )

    greet(n, chips, True)

    def produce(t):
        slots = pl.ds(n - (t + 1) * batch, batch)
        rows_in = gated_ref[slots].reshape(batch * rows, gated_ref.shape[2])
        tile = 768
        for start in range(0, part_ref.shape[2], tile):
            part = slice(start, start + tile)
            value = jnp.dot(rows_in, down_ref[:, part], preferred_element_type=jnp.float32)
            part_ref[slots, :, part] = value.astype(jnp.bfloat16).reshape(batch, rows, tile)
        for e in range(batch):
            for j in list(range(1, chips)) + [0]:
                swap(t * batch + e, j).start()

    def paired(i, j):
        swap(i, j).wait_recv()
        head = pl.multiple_of((column(j) * 2 + core) * width, 128)
        own = part_ref[n - 1 - i, :, pl.ds(head, width)]
        return own.astype(jnp.float32) + pair[i, j].astype(jnp.float32)

    def first(i):
        for j in range(1, chips):
            out_x[i, j] = paired(i, j).astype(jnp.bfloat16)
            cross(i, j).start()

    def second(i):
        acc = paired(i, 0)
        for j in range(1, chips):
            cross(i, j).wait_recv()
            acc = acc + in_x[i, j].astype(jnp.float32)
        total[i] = acc.astype(jnp.bfloat16)

    groups = n // batch
    produce(0)

    @pl.loop(0, groups)
    def _(t):
        @pl.when(t + 1 < groups)
        def _():
            produce(t + 1)

        for e in range(batch):
            first(t * batch + e)

        @pl.when(t >= 1)
        def _():
            for e in range(batch):
                second((t - 1) * batch + e)
                home((t - 1) * batch + e).start()

    for i in range(n - batch, n):
        second(i)
        if i < n - 1:
            home(i).start()
    keep = pltpu.make_async_copy(total.at[n - 1], ret_ref.at[me], here)
    keep.start()

    @pl.loop(0, n - 1)
    def _(i):
        back = lax.rem(me - 1 - i + n, n)
        remote(total.at[i], ret_ref.at[back], a_s.at[i], a_r.at[i], me, mine).wait_recv()
        home(i).wait_send()

    @pl.loop(0, n)
    def _(i):
        for j in range(chips):
            swap(i, j).wait_send()
        for j in range(1, chips):
            cross(i, j).wait_send()

    keep.wait()


def giveback(gated, down, n, heads):
    chips = heads // 2
    rows, width = gated.shape[1], down.shape[1] // heads
    dma = pltpu.SemaphoreType.DMA
    piece = pltpu.VMEM((n, chips, rows, width), jnp.bfloat16)
    return pl.pallas_call(
        functools.partial(giveback_kernel, n, chips, 2 if rows % 16 == 0 else 1),
        out_shape=jax.ShapeDtypeStruct((n, rows, width), jnp.bfloat16),
        in_specs=[pl.BlockSpec(memory_space=pltpu.VMEM)] * 2,
        out_specs=pl.BlockSpec(memory_space=pl.ANY),
        scratch_shapes=[
            pltpu.VMEM((n, rows, width * heads), jnp.bfloat16),
            piece,
            piece,
            piece,
            pltpu.VMEM((n, rows, width), jnp.bfloat16),
        ]
        + [dma]
        + [dma((chips, n))] * 4
        + [dma((n,))] * 2,
        compiler_params=pltpu.CompilerParams(
            collective_id=1, has_side_effects=True, vmem_limit_bytes=60 * 1024 * 1024
        ),
        name="giveback",
    )(gated, down)


def attend_kernel(
    n,
    heads,
    q_ref,
    k_ref,
    v_ref,
    allowed_ref,
    keep_ref,
    carry_ref,
    earlier_ref,
    gain_ref,
    w_ref,
    res_ref,
    hidden_ref,
    squares_ref,
    wall,
    states,
    attn,
    headed,
    acc,
    mixed,
    pair,
    out_x,
    in_x,
    sq_own,
    sq_all,
    here,
    w_s,
    w_r,
    s_s,
    s_r,
    p_s,
    p_r,
    x_s,
    x_r,
    q_s,
    q_r,
):
    me, chip, core = seat()
    chips = heads // 2
    mine, partner = chip * 2 + core, chip * 2 + 1 - core
    local, size = states.shape[1], HEAD_DIM
    half, piece = w_ref.shape[0] // 2, w_ref.shape[0] // 4
    group = n // heads
    f32 = jnp.float32

    def seat_at(p):
        return 2 * p - lax.div(p, n // 2) * (4 * p - 2 * n + 1)

    low = lax.div(me, 2)
    place = low + lax.rem(me, 2) * (n - lax.div(me + 1, 2) - low)
    ahead = [seat_at(lax.rem(place + 1, n)), seat_at(lax.rem(place + n - 1, n))]

    def origin(way, distance):
        step = n - distance if way == 0 else distance
        return seat_at(lax.rem(place + step, n))

    barrier = pltpu.get_barrier_semaphore()

    def tell(ctx, head):
        pl.semaphore_signal(barrier, inc=1, device_id=(ctx, head), device_id_type=MESH)

    tell(ahead[0], mine)
    tell(ahead[1], mine)
    for j in range(1, heads):
        tell(me, lax.rem(mine + j, heads))
    pl.semaphore_wait(barrier, heads + 1)

    def w_rows(way, part):
        return pl.ds(way * half + part * piece, piece)

    def w_first(way, part):
        rows = w_rows(way, part)
        return remote(
            w_ref.at[rows],
            wall.at[me, rows],
            w_s.at[way, part, 0],
            w_r.at[way, part, 0],
            ahead[way],
            mine,
        )

    def w_step(way, part, held, stage):
        cell = wall.at[origin(way, held), w_rows(way, part)]
        return remote(
            cell, cell, w_s.at[way, part, stage], w_r.at[way, part, stage], ahead[way], mine
        )

    def s_step(way, held, stage):
        cell = states.at[origin(way, held), pl.ds(way * (local // 2), local // 2)]
        return remote(cell, cell, s_s.at[way, stage], s_r.at[way, stage], ahead[way], mine)

    for part in range(2):
        for way in range(2):
            w_first(way, part).start()
    own = pltpu.make_async_copy(w_ref, wall.at[me], here)
    own.start()

    def columns(h):
        return pl.ds(pl.multiple_of(h * size, size), size)

    def lifted(ref, h):
        x = ref[:, columns(h)].astype(f32)
        return x / (1.0 + jnp.exp(-x))

    @pl.loop(0, local)
    def _(h):
        kept = lifted(k_ref, h) * keep_ref[...]
        state = jnp.dot(
            kept.T, v_ref[:, columns(h)].astype(f32), precision=highest, preferred_element_type=f32
        )
        states[me, h] = state.astype(jnp.bfloat16)

    for way in range(2):
        s_step(way, 0, 0).start()

    @pl.loop(0, local)
    def _(h):
        scores = lax.dot_general(
            lifted(q_ref, h),
            lifted(k_ref, h),
            (((1,), (1,)), ((), ())),
            precision=highest,
            preferred_element_type=f32,
        )
        attn[:, columns(h)] = jnp.dot(
            scores * allowed_ref[...],
            v_ref[:, columns(h)].astype(f32),
            precision=highest,
            preferred_element_type=f32,
        )

    acc[...] = jnp.zeros_like(acc)

    def s_stage(stage):
        for way in range(2):
            s_step(way, stage + 1, stage).wait_recv()

            @pl.when(stage < n - 2)
            def _():
                s_step(way, stage + 1, stage + 1).start()

    def w_stage(stage):
        for part in range(2):
            for way in range(2):
                w_step(way, part, stage + 1, stage).wait_recv()

                @pl.when(stage < n - 2)
                def _():
                    w_step(way, part, stage + 1, stage + 1).start()

    early = (n - 2) // 2

    @pl.loop(0, early)
    def _(t):
        s_stage(2 * t)
        s_stage(2 * t + 1)
        w_stage(t)

    s_stage(n - 2)

    @pl.loop(0, local)
    def _(h):
        def add(j, total):
            return total + earlier_ref[j] * states[j, h].astype(f32)

        state = lax.fori_loop(0, n, add, jnp.zeros((size, size), f32))
        outside = jnp.dot(
            lifted(q_ref, h), state, precision=highest, preferred_element_type=f32
        )
        full = attn[:, columns(h)] + outside * carry_ref[...]
        mean_square = jnp.mean(full * full, axis=1, keepdims=True)
        scaled = full * lax.rsqrt(mean_square + 1e-06) * gain_ref[:, columns(h)]
        headed[:, columns(h)] = scaled.astype(jnp.bfloat16)

    def project(way, held):
        src = origin(way, held)
        rows = pl.ds(way * half, half)
        acc[src] += jnp.dot(headed[:, rows], wall[src, rows], preferred_element_type=f32)

    own.wait()

    @pl.loop(0, early + 1)
    def _(held):
        project(0, held)
        project(1, held)

    @pl.loop(early, n - 1)
    def _(stage):
        w_stage(stage)
        project(0, stage + 1)
        project(1, stage + 1)

    mixed[...] = acc[...].astype(jnp.bfloat16)

    def column(j):
        return lax.rem(chip + j, chips)

    def blocks(head):
        return pl.ds(head * group, group)

    def swap(j):
        return remote(
            mixed.at[blocks(column(j) * 2 + 1 - core)],
            pair.at[j],
            p_s.at[j],
            p_r.at[j],
            me,
            partner,
        )

    def cross(j):
        return remote(
            out_x.at[j], in_x.at[j], x_s.at[j], x_r.at[j], me, column(j) * 2 + core
        )

    for j in list(range(1, chips)) + [0]:
        swap(j).start()

    def paired(j):
        swap(j).wait_recv()
        return acc[blocks(column(j) * 2 + core)] + pair[j].astype(f32)

    for j in range(1, chips):
        out_x[j] = paired(j).astype(jnp.bfloat16)
        cross(j).start()
    total = paired(0) + res_ref[...].astype(f32)
    hidden_ref[...] = total
    for j in range(1, chips):
        cross(j).wait_recv()
        hidden_ref[...] += in_x[j].astype(f32)
    ones = jnp.ones((8, hidden_ref.shape[2]), f32)
    squares = jnp.zeros((8, hidden_ref.shape[1]), f32)
    for b in range(group):
        part = hidden_ref[b]
        squares = squares + lax.dot_general(
            ones,
            part * part,
            (((1,), (1,)), ((), ())),
            precision=highest,
            preferred_element_type=f32,
        )
    sq_own[...] = squares

    def share(j, to, slot):
        return remote(sq_own, sq_all.at[slot], q_s.at[j], q_r.at[j], me, to)

    for j in range(1, heads):
        share(j, lax.rem(mine + j, heads), j).start()
    for j in range(1, heads):
        share(j, mine, j).wait_recv()
        squares = squares + sq_all[j]
    squares_ref[...] = squares

    for j in range(1, heads):
        share(j, mine, j).wait_send()
    for j in range(chips):
        swap(j).wait_send()
    for j in range(1, chips):
        cross(j).wait_send()

    for part in range(2):
        for way in range(2):
            w_first(way, part).wait_send()

    @pl.loop(0, n - 1)
    def _(stage):
        for way in range(2):
            s_step(way, stage, stage).wait_send()

    @pl.loop(1, n - 1)
    def _(stage):
        for part in range(2):
            for way in range(2):
                w_step(way, part, stage, stage).wait_send()


def attend(query, key, value, allowed, keep, carry, earlier, gain, weight, residual, n, heads):
    rows, feats = query.shape
    width, group = weight.shape[1], n // heads
    local, chips = feats // HEAD_DIM, heads // 2
    dma = pltpu.SemaphoreType.DMA
    bf16, f32 = jnp.bfloat16, jnp.float32
    vmem = pl.BlockSpec(memory_space=pltpu.VMEM)
    piece = pltpu.VMEM((chips, group, rows, width), bf16)
    return pl.pallas_call(
        functools.partial(attend_kernel, n, heads),
        out_shape=(
            jax.ShapeDtypeStruct((group, rows, width), f32),
            jax.ShapeDtypeStruct((8, rows), f32),
        ),
        in_specs=[vmem] * 8 + [pl.BlockSpec(memory_space=pl.ANY), vmem],
        out_specs=(vmem, vmem),
        scratch_shapes=[
            pltpu.VMEM((n,) + weight.shape, bf16),
            pltpu.VMEM((n, local, HEAD_DIM, HEAD_DIM), bf16),
            pltpu.VMEM((rows, feats), f32),
            pltpu.VMEM((rows, feats), bf16),
            pltpu.VMEM((n, rows, width), f32),
            pltpu.VMEM((n, rows, width), bf16),
            piece,
            piece,
            piece,
            pltpu.VMEM((8, rows), f32),
            pltpu.VMEM((heads, 8, rows), f32),
            dma,
            dma((2, 2, n)),
            dma((2, 2, n)),
            dma((2, n)),
            dma((2, n)),
            dma((chips,)),
            dma((chips,)),
            dma((chips,)),
            dma((chips,)),
            dma((heads,)),
            dma((heads,)),
        ],
        compiler_params=pltpu.CompilerParams(
            collective_id=2, has_side_effects=True, vmem_limit_bytes=60 * 1024 * 1024
        ),
        name="attend",
    )(query, key, value, allowed, keep, carry, earlier, gain, weight, residual)


def episode_of(positions, lengths):
    starts = jnp.cumsum(lengths) - lengths
    return jnp.sum((starts[None, :] <= positions[:, None]).astype(jnp.int32), axis=1) - 1


def on_device(
    query,
    key,
    value,
    episode_lengths,
    attn_gain,
    out_weight,
    residual,
    norm_gain,
    expert_ids,
    route_weights,
    gate_weight,
    up_weight,
    down_weight,
):
    tok_rows = query.shape[0]
    head_size = HEAD_DIM
    own_index = lax.axis_index("ctx")
    ctx_count = lax.axis_size("ctx")
    positions = own_index * tok_rows + jnp.arange(tok_rows, dtype=jnp.int32)
    episode = episode_of(positions, episode_lengths)
    prior = episode_of(positions[:1] - 1, episode_lengths)[0]
    final = episode[-1]
    keep = (episode == final).astype(jnp.float32)
    finals = episode_of(
        (jnp.arange(ctx_count, dtype=jnp.int32) + 1) * tok_rows - 1, episode_lengths
    )
    earlier = (jnp.arange(ctx_count) < own_index) & (finals == prior)
    earlier = jnp.broadcast_to(
        earlier.astype(jnp.float32)[:, None, None], (ctx_count, 1, head_size)
    )
    order = jnp.arange(tok_rows, dtype=jnp.int32)
    allowed = ((order[:, None] >= order[None, :]) & (episode[:, None] == episode[None, :])).astype(
        jnp.float32
    )
    heads = lax.axis_size("head")
    col = out_weight.shape[1]
    width = residual.shape[1] * heads
    hidden_blocks, squares = attend(
        query,
        key,
        value,
        allowed,
        keep[:, None],
        (episode == prior).astype(jnp.float32)[:, None],
        earlier,
        attn_gain[None, :],
        out_weight,
        jnp.swapaxes(residual.reshape(tok_rows, -1, col), 0, 1),
        ctx_count,
        heads,
    )
    hidden_slice = jnp.swapaxes(hidden_blocks, 0, 1).reshape(tok_rows, -1)
    normed = (
        hidden_slice * lax.rsqrt(squares[0] / width + 1e-06)[:, None] * norm_gain
    ).astype(jnp.bfloat16)
    experts_count = gate_weight.shape[0] * ctx_count
    capacity = 3 * tok_rows // experts_count
    flat_ids = expert_ids.reshape(-1)
    onehot = (flat_ids[:, None] == jnp.arange(experts_count, dtype=jnp.int32)[None, :]).astype(
        jnp.int32
    )
    slot = jnp.sum(jnp.cumsum(onehot, axis=0) * onehot, axis=1) - 1
    target = (flat_ids * capacity + slot).reshape(tok_rows, 2)
    places = jnp.arange(experts_count * capacity, dtype=jnp.int32)
    spread = (
        (places[:, None] == target[None, :, 0]) | (places[:, None] == target[None, :, 1])
    ).astype(jnp.bfloat16)
    outgoing = (
        jnp.dot(spread, normed, preferred_element_type=jnp.float32)
        .astype(jnp.bfloat16)
        .reshape(experts_count, capacity, normed.shape[1])
    )
    raw_weights = route_weights.astype(jnp.float32)
    share = raw_weights / jnp.sum(raw_weights, axis=1, keepdims=True)
    gated = dispatch(outgoing, gate_weight[0], up_weight[0], ctx_count, heads)
    returned = giveback(gated, down_weight[0], ctx_count, heads)
    returned = returned.reshape(-1, returned.shape[2])
    moe = 0.0
    for k in range(2):
        pick = (target[:, k : k + 1] == places[None, :]).astype(jnp.bfloat16)
        moe = moe + share[:, k : k + 1] * jnp.dot(
            pick, returned, preferred_element_type=jnp.float32
        )
    return (hidden_slice + moe).astype(jnp.bfloat16)


def solution(mesh):
    placed = (
        P("ctx", "head"),
        P("ctx", "head"),
        P("ctx", "head"),
        P(),
        P("head"),
        P("head", "ctx"),
        P("ctx", "head"),
        P("head"),
        P("ctx", None),
        P("ctx", None),
        P("ctx", None, "head"),
        P("ctx", None, "head"),
        P("ctx", "head", None),
    )
    return jax.shard_map(
        on_device, mesh=mesh, in_specs=placed, out_specs=P("ctx", "head"), check_vma=False
    )
```
